32 devices in a mesh: wide: 8 (over z, x), narrow: 4 (over y, core).
Axes of the slice: x: 2, y: 2, z: 4, core: 2. Of those that a mesh axis runs over, the one named last changes fastest.
Arguments:
- moments: float32 [4096, 2048], P('wide', 'narrow'), as said below
- eigen_basis: float32 [4096, 2048], P('wide', 'narrow'), may hold values from -0.125 to 0.125
- slot_order: int32 [2], replicated, may hold values 0 or 1
Outputs:
- halves: float32 [4096, 1024], P('wide', 'narrow')
The draws below stay inside these ranges and needn't reach their ends.
Inputs may be any that keep to these rules, and one draw needn't show every extreme that they name: Each block of 2048 rows of moments is symmetric.
All inputs are finite; a program needn't handle non-finite values.
Results may differ from the reference program's by a relative error of at most 0.0001.
Values sent between devices are 32-bit elements; how exact they have to be, the bound alone decides.
A program may use at most 64 MiB of HBM per device.

```python
import jax
import jax.numpy as jnp
from jax import lax

M = 2048
K = 1024
GROUPS = 2


def draw_moments(key, part):
    base_key = jax.random.fold_in(jax.random.fold_in(key, 11), 0)
    entries = jax.random.normal(base_key, (GROUPS, M, M), jnp.float32)
    symmetric = (entries + jnp.swapaxes(entries, 1, 2)) * 0.7071
    return symmetric.reshape(GROUPS * M, M)


def with_ends(values, rng, least, top_value):
    place = [jax.random.randint(jax.random.fold_in(rng, axis), (), 0, length) for axis, length in enumerate(values.shape)]
    longest = values.shape.index(max(values.shape))
    beside = place[:longest] + [(place[longest] + 1) % values.shape[longest]] + place[longest + 1:]
    return values.at[tuple(place)].set(least).at[tuple(beside)].set(top_value)


def block_scale(stream_key, dims, cuts, low, largest):
    gain = 1.0
    for position, blocks in cuts:
        heights = jax.random.uniform(jax.random.fold_in(jax.random.fold_in(stream_key, 6), position), (blocks,), jnp.float32, low / len(cuts), largest / len(cuts))
        gain = gain * jnp.repeat(jnp.exp(heights), dims[position] // blocks).reshape((-1,) + (1,) * (len(dims) - 1 - position))
    return gain


def gaussian(own_key, dims, scale, limit, pieces=(), held_as=jnp.bfloat16):
    values = jax.random.normal(own_key, dims, jnp.float32) * scale
    if len(pieces) > 0:
        values = block_scale(own_key, dims, pieces, -0.22, 0.18) * values
    return jnp.clip(values, min=-limit, max=limit).astype(held_as)


def setup_inputs(seed: int = 0) -> dict:
    key_list = jax.random.split(jax.random.key(seed), 4)
    return {
        "moments": draw_moments(jax.random.fold_in(key_list[3], 71), 0),
        "eigen_basis": gaussian(key_list[1], (GROUPS * M, M), M ** -0.5, 0.125, ((0, 8), (1, 4)), jnp.float32),
        "slot_order": with_ends((jax.random.randint(key_list[2], (GROUPS,), 0, 2) < 1).astype(jnp.int32), jax.random.fold_in(key_list[2], 1), 0, 1),
    }


def reference(moments, eigen_basis, slot_order):
    outputs = []
    for subproblem in range(GROUPS):
        matrix = moments[subproblem * M:(subproblem + 1) * M]
        vectors = eigen_basis[subproblem * M:(subproblem + 1) * M]
        product = jnp.dot(matrix, vectors, precision=lax.Precision.HIGHEST, preferred_element_type=jnp.float32)
        first_block = jnp.dot(vectors[:, :K].T, product[:, :K], precision=lax.Precision.HIGHEST, preferred_element_type=jnp.float32)
        second = jnp.dot(vectors[:, K:].T, product[:, K:], precision=lax.Precision.HIGHEST, preferred_element_type=jnp.float32)
        swapped = slot_order[subproblem] == 1
        outputs.append(jnp.where(swapped, second, first_block))
        outputs.append(jnp.where(swapped, first_block, second))
    return jnp.concatenate(outputs, axis=0)
```

```python
import jax
import jax.numpy as jnp
from jax import lax
from jax.experimental import pallas as pl
from jax.experimental.pallas import tpu as pltpu
from jax.sharding import PartitionSpec as P

GROUP_WIDE = 4
K = 1024
MESH = pl.DeviceIdType.MESH
CHUNKS = 4


def split(value):
    high = value.astype(jnp.bfloat16)
    low = (value - high.astype(jnp.float32)).astype(jnp.bfloat16)
    return high, low


def dot3(left, right):
    def dot(a, b):
        return jnp.dot(a, b, preferred_element_type=jnp.float32)

    return dot(left[0], right[0]) + (dot(left[0], right[1]) + dot(left[1], right[0]))


def kernel(
    slot_ref, a_ref, v_ref, o_ref,
    abuf, vbuf, left, left_t, acc, csend, cmine, crecv, sums, gsame, gother, zsend, zrecv,
    local_sem, send_sem, recv_sem, extra_sem,
):
    rows, cols = a_ref.shape
    half = rows // 2
    chunk = csend.shape[1]
    w = lax.axis_index("wide")
    n = lax.axis_index("narrow")
    x = w % 2
    z = (w // 2) % 2
    y = n // 2
    core = n % 2
    p = w % 4
    wx = w + 1 - 2 * x
    wz = w + 2 - 4 * z
    px = p + 1 - 2 * x
    pz = p + 2 - 4 * z
    pd = 3 - p
    ns = n + 1 - 2 * core
    ny = n + 2 - 4 * y
    nd = 3 - n
    q = 2 * y + core

    barrier = pltpu.get_barrier_semaphore()
    for target in ((wx, n), (wz, n), (w, ns), (w, ny), (w, nd)):
        pl.semaphore_signal(barrier, inc=1, device_id=target, device_id_type=MESH)

    local = [
        pltpu.make_async_copy(v_ref, vbuf.at[p], local_sem.at[0]),
        pltpu.make_async_copy(v_ref, left.at[core], local_sem.at[1]),
        pltpu.make_async_copy(a_ref, abuf.at[q], local_sem.at[2]),
    ]
    for copy in local:
        copy.start()

    used = []

    def remote(src, dst, target):
        index = len(used)
        used.append(index)
        return pltpu.make_async_remote_copy(
            src_ref=src, dst_ref=dst, send_sem=send_sem.at[index], recv_sem=recv_sem.at[index],
            device_id=target, device_id_type=MESH,
        )

    top, bottom = pl.ds(0, half), pl.ds(half, half)
    vx = [remote(v_ref.at[part], vbuf.at[p, part], (wx, n)) for part in (top, bottom)]
    vz = [remote(v_ref.at[part], vbuf.at[p, part], (wz, n)) for part in (bottom, top)]
    ay = [remote(a_ref.at[part], abuf.at[q, part], (w, ny)) for part in (top, bottom)]
    vs = remote(v_ref, left.at[core], (w, ns))
    as_ = remote(a_ref, abuf.at[q], (w, ns))
    qy = 2 * (1 - y) + core
    vxr = remote(vbuf.at[px, top], vbuf.at[px, top], (wz, n))
    vzr = remote(vbuf.at[pz, bottom], vbuf.at[pz, bottom], (wx, n))
    ayr = [remote(abuf.at[qy, part], abuf.at[qy, part], (w, ns)) for part in (top, bottom)]

    pl.semaphore_wait(barrier, 5)
    for copy in (vx[0], vz[0], ay[0], vx[1], vz[1], ay[1], vs, as_):
        copy.start()
    for copy in local:
        copy.wait()
    left_t[core, 0], left_t[core, 1] = split(left[core].T)
    vx[0].wait_recv()
    vxr.start()
    vz[0].wait_recv()
    vzr.start()
    ay[0].wait_recv()
    ayr[0].start()
    vs.wait_recv()
    left_t[1 - core, 0], left_t[1 - core, 1] = split(left[1 - core].T)
    ay[1].wait_recv()
    ayr[1].start()
    as_.wait_recv()
    ayr[0].wait_recv()
    ayr[1].wait_recv()
    acc[...] = dot3(split(abuf[p]), split(vbuf[p]))
    vx[1].wait_recv()
    acc[...] += dot3(split(abuf[px]), split(vbuf[px]))
    vz[1].wait_recv()
    acc[...] += dot3(split(abuf[pz]), split(vbuf[pz]))
    vxr.wait_recv()
    vzr.wait_recv()
    acc[...] += dot3(split(abuf[pd]), split(vbuf[pd]))

    image = split(acc[...])
    cx = [remote(csend.at[j], crecv.at[j], (wx, n)) for j in range(CHUNKS)]
    for j in range(0, CHUNKS, 2):
        part = pl.ds(j * chunk, 2 * chunk)
        block = dot3((left_t[1 - x, 0, part], left_t[1 - x, 1, part]), image)
        csend[j] = block[:chunk]
        csend[j + 1] = block[chunk:]
        cx[j].start()
        cx[j + 1].start()
    for j in range(0, CHUNKS, 2):
        part = pl.ds(j * chunk, 2 * chunk)
        block = dot3((left_t[x, 0, part], left_t[x, 1, part]), image)
        cmine[j] = block[:chunk]
        cmine[j + 1] = block[chunk:]

    stays = core == y
    leaves = core != y
    keep = [remote(sums.at[j, 1 - core], gsame.at[j], (w, ns)) for j in range(CHUNKS)]
    cross = [remote(sums.at[j, core], gother.at[j], (w, ny)) for j in range(CHUNKS)]
    first = len(used) - CHUNKS
    cross_d = [
        pltpu.make_async_remote_copy(
            src_ref=sums.at[j, 1 - core], dst_ref=gother.at[j],
            send_sem=extra_sem.at[j], recv_sem=recv_sem.at[first + j],
            device_id=(w, nd), device_id_type=MESH,
        )
        for j in range(CHUNKS)
    ]
    zc = [remote(zsend.at[j], zrecv.at[j], (wz, n)) for j in range(CHUNKS)]

    swapped = slot_ref[w // GROUP_WIDE]
    wide_half = gsame.shape[2]
    same_flag = ((z + swapped + y) % 2) == 0

    def reduce_x(j):
        cx[j].wait_recv()
        for k in range(2):
            piece = pl.ds(k * wide_half, wide_half)
            sums[j, k] = cmine[j, :, piece] + crecv[j, :, piece]

        @pl.when(stays)
        def _():
            keep[j].start()
            gsame[j] = sums[j, core]

        @pl.when(leaves)
        def _():
            cross[j].start()
            cross_d[j].start()

    def select_z(j):
        @pl.when(leaves)
        def _():
            keep[j].wait_recv()

        cross[j].wait_recv()
        same, other = gsame[j], gother[j]
        mask = jnp.full(same.shape, same_flag.astype(jnp.int32)) == 1
        zsend[j] = jnp.where(mask, other, same)
        zc[j].start()
        o_ref[pl.ds(j * chunk, chunk), :] = jnp.where(mask, same, other)

    def finish(j):
        zc[j].wait_recv()
        o_ref[pl.ds(j * chunk, chunk), :] += zrecv[j]

    for step in range(CHUNKS + 2):
        if step < CHUNKS:
            reduce_x(step)
        if 0 <= step - 1 < CHUNKS:
            select_z(step - 1)
        if 0 <= step - 2 < CHUNKS:
            finish(step - 2)

    for copy in (*vx, *vz, *ay, vs, as_, vxr, vzr, *ayr, *cx, *zc):
        copy.wait_send()

    @pl.when(stays)
    def _():
        for copy in keep:
            copy.wait_send()

    @pl.when(leaves)
    def _():
        for copy in (*cross, *cross_d):
            copy.wait_send()


def fast_body(moments, eigen_basis, slot_order):
    rows, cols = moments.shape
    f32 = jnp.float32
    chunk = rows // CHUNKS
    return pl.pallas_call(
        kernel,
        out_shape=jax.ShapeDtypeStruct((rows, cols // 2), f32),
        in_specs=[
            pl.BlockSpec(memory_space=pltpu.SMEM),
            pl.BlockSpec(memory_space=pl.ANY),
            pl.BlockSpec(memory_space=pl.ANY),
        ],
        out_specs=pl.BlockSpec(memory_space=pltpu.VMEM),
        scratch_shapes=[
            pltpu.VMEM((4, rows, cols), f32),
            pltpu.VMEM((4, rows, cols), f32),
            pltpu.VMEM((2, rows, cols), f32),
            pltpu.VMEM((2, 2, cols, rows), jnp.bfloat16),
            pltpu.VMEM((rows, cols), f32),
            pltpu.VMEM((CHUNKS, chunk, cols), f32),
            pltpu.VMEM((CHUNKS, chunk, cols), f32),
            pltpu.VMEM((CHUNKS, chunk, cols), f32),
            pltpu.VMEM((CHUNKS, 2, chunk, cols // 2), f32),
            pltpu.VMEM((CHUNKS, chunk, cols // 2), f32),
            pltpu.VMEM((CHUNKS, chunk, cols // 2), f32),
            pltpu.VMEM((CHUNKS, chunk, cols // 2), f32),
            pltpu.VMEM((CHUNKS, chunk, cols // 2), f32),
            pltpu.SemaphoreType.DMA((3,)),
            pltpu.SemaphoreType.DMA((40,)),
            pltpu.SemaphoreType.DMA((40,)),
            pltpu.SemaphoreType.DMA((CHUNKS,)),
        ],
        compiler_params=pltpu.CompilerParams(
            collective_id=0, has_side_effects=True, vmem_limit_bytes=56 * 1024 * 1024
        ),
        name="rayleigh",
    )(slot_order, moments, eigen_basis)


def partner(value, axis, stride):
    mask = 2**stride
    pairs = [(source, source ^ mask) for source in range(lax.axis_size(axis))]
    return lax.ppermute(value, axis, pairs)


def body(moments, eigen_basis, slot_order):
    wide_pos = lax.axis_index("wide")
    subproblem = wide_pos // GROUP_WIDE
    position = wide_pos % GROUP_WIDE
    swapped = lax.dynamic_index_in_dim(slot_order, subproblem, 0, keepdims=False)
    narrow_pos = lax.axis_index("narrow")
    col_count = eigen_basis.shape[1]
    half_cols = col_count // 2
    full_basis = lax.all_gather(eigen_basis, "narrow", axis=1, tiled=True)
    first_half = lax.dynamic_slice_in_dim(full_basis, narrow_pos * half_cols, half_cols, 1)
    second_half = lax.dynamic_slice_in_dim(full_basis, K + narrow_pos * half_cols, half_cols, 1)
    local_panel = jnp.concatenate([first_half, second_half], axis=1)
    pair_block = partner(local_panel, "wide", 0)
    joined = jnp.where(
        position % 2 == 0,
        jnp.concatenate([local_panel, pair_block], axis=0),
        jnp.concatenate([pair_block, local_panel], axis=0),
    )
    quad_block = partner(joined, "wide", 1)
    col_panel = jnp.where(
        position // 2 % 2 == 0,
        jnp.concatenate([joined, quad_block], axis=0),
        jnp.concatenate([quad_block, joined], axis=0),
    )
    products = jnp.dot(
        lax.all_gather(moments, "narrow", axis=1, tiled=True),
        col_panel,
        precision=lax.Precision.HIGHEST,
        preferred_element_type=jnp.float32,
    )
    partials = []
    for slot_index in range(2):
        half_panel = products[:, slot_index * half_cols : (slot_index + 1) * half_cols]
        vectors_half = full_basis[:, slot_index * K : (slot_index + 1) * K]
        partials.append(
            lax.dot_general(
                vectors_half,
                half_panel,
                (((0,), (0,)), ((), ())),
                precision=lax.Precision.HIGHEST,
                preferred_element_type=jnp.float32,
            )
        )
    stacked = jnp.stack(partials)
    slot_pick = (position // 2 + swapped) % 2
    row_part = position % 2
    summed = stacked + partner(stacked, "wide", 0)
    summed = summed + partner(summed, "wide", 1)
    chosen = lax.dynamic_index_in_dim(summed, slot_pick, 0, keepdims=False)
    return lax.dynamic_slice_in_dim(chosen, row_part * (K // 2), K // 2, 0)


def solution(mesh):
    placed = (P("wide", "narrow"), P("wide", "narrow"), P())
    cube = mesh.shape["narrow"] == 4
    return jax.shard_map(
        fast_body if cube else body, mesh=mesh, in_specs=placed, out_specs=P("wide", "narrow"), check_vma=False
    )
```

```python
import jax
import jax.numpy as jnp
from jax import lax
from jax.experimental import pallas as pl
from jax.experimental.pallas import tpu as pltpu
from jax.sharding import PartitionSpec as P

GROUP_WIDE = 4
K = 1024
MESH = pl.DeviceIdType.MESH
CHUNKS = 4
PIECES = 4
RELAYED = 3
COPIES = 8 * PIECES + 7 * CHUNKS + 2


def split(value):
    high = value.astype(jnp.bfloat16)
    low = (value - high.astype(jnp.float32)).astype(jnp.bfloat16)
    return high, low


def dot3(left, right):
    def dot(a, b):
        return jnp.dot(a, b, preferred_element_type=jnp.float32)

    return dot(left[0], right[0]) + (dot(left[0], right[1]) + dot(left[1], right[0]))


def kernel(
    slot_ref, a_ref, v_ref, o_ref,
    abuf, aparts, vbuf, left, left_t, csend, cmine, crecv, sums, gsame, gother, zsend, zrecv,
    local_sem, send_sem, recv_sem,
):
    rows, cols = a_ref.shape
    wide_half = cols // 2
    piece = rows // PIECES
    chunk = rows // CHUNKS
    w = lax.axis_index("wide")
    n = lax.axis_index("narrow")
    x = w % 2
    z = (w // 2) % 2
    y = n // 2
    core = n % 2
    p = w % 4
    wx = w + 1 - 2 * x
    wz = w + 2 - 4 * z
    px = p + 1 - 2 * x
    pz = p + 2 - 4 * z
    pd = 3 - p
    ns = n + 1 - 2 * core
    ny = n + 2 - 4 * y
    nd = 3 - n
    q = 2 * y + core
    qs = 2 * y + 1 - core
    qy = 2 * (1 - y) + core
    qd = 3 - q

    barrier = pltpu.get_barrier_semaphore()
    for target in ((wx, n), (wz, n), (w, ns), (w, ny), (w, nd)):
        pl.semaphore_signal(barrier, inc=1, device_id=target, device_id_type=MESH)

    def part(i):
        return pl.ds(i * piece, piece)

    def side(t):
        return pl.ds(t * wide_half, wide_half)

    local = [
        pltpu.make_async_copy(v_ref, left.at[core], local_sem.at[0]),
        pltpu.make_async_copy(a_ref, abuf.at[q], local_sem.at[1]),
        pltpu.make_async_copy(v_ref.at[:, side(0)], vbuf.at[p, 0], local_sem.at[2]),
        pltpu.make_async_copy(v_ref.at[:, side(1)], vbuf.at[p, 1], local_sem.at[3]),
    ]
    for copy in local:
        copy.start()

    used = []

    def remote(src, dst, target):
        index = len(used)
        used.append(index)
        return pltpu.make_async_remote_copy(
            src_ref=src, dst_ref=dst, send_sem=send_sem.at[index], recv_sem=recv_sem.at[index],
            device_id=target, device_id_type=MESH,
        )

    def own(t, i, target):
        return remote(v_ref.at[part(i), side(t)], vbuf.at[p, t, part(i)], target)

    def relay(t, i, block, target):
        return remote(vbuf.at[block, t, part(i)], vbuf.at[block, t, part(i)], target)

    vx = [[own(t, i, (wx, n)) for i in range(PIECES)] for t in range(2)]
    vz = [[own(t, i, (wz, n)) for i in range(PIECES)] for t in range(2)]
    vxr = [[relay(t, i, px, (wz, n)) for i in range(RELAYED)] for t in range(2)]
    vzr = [[relay(t, i, pz, (wx, n)) for i in range(RELAYED, PIECES)] for t in range(2)]
    ay = [remote(a_ref.at[part(i)], abuf.at[q, part(i)], (w, ny)) for i in range(PIECES)]
    ayr = [remote(abuf.at[qy, part(i)], abuf.at[qy, part(i)], (w, ns)) for i in range(PIECES)]
    vs = remote(v_ref, left.at[core], (w, ns))
    as_ = remote(a_ref, abuf.at[q], (w, ns))
    cx = [[remote(csend.at[t, j], crecv.at[t, j], (wx, n)) for j in range(CHUNKS)] for t in range(2)]
    keep = [[remote(sums.at[t, j], gsame.at[j], (w, ns)) for j in range(CHUNKS)] for t in range(2)]
    cross = [[remote(sums.at[t, j], gother.at[j], (w, 2 * (1 - y) + t)) for j in range(CHUNKS)] for t in range(2)]
    zc = [remote(zsend.at[j], zrecv.at[j], (wz, n)) for j in range(CHUNKS)]

    def start_own(t):
        for i in range(PIECES):
            vx[t][i].start()
            vz[t][PIECES - 1 - i].start()

    def start_relays(t):
        late = list(range(RELAYED, PIECES))[::-1]
        for i in range(max(RELAYED, PIECES - RELAYED)):
            if i < RELAYED:
                vx[t][i].wait_recv()
                vxr[t][i].start()
            if i < PIECES - RELAYED:
                vz[t][late[i]].wait_recv()
                vzr[t][late[i] - RELAYED].start()

    pl.semaphore_wait(barrier, 5)
    start_own(0)
    for copy in (*ay, vs, as_):
        copy.start()
    for copy in local:
        copy.wait()
    start_relays(0)
    start_own(1)
    ay[0].wait_recv()
    ayr[0].start()
    aparts[q, 0], aparts[q, 1] = split(abuf[q])
    left_t[core, 0], left_t[core, 1] = split(left[core].T)
    ay[1].wait_recv()
    ayr[1].start()
    vs.wait_recv()
    left_t[1 - core, 0], left_t[1 - core, 1] = split(left[1 - core].T)
    as_.wait_recv()
    aparts[qs, 0], aparts[qs, 1] = split(abuf[qs])
    ay[2].wait_recv()
    ayr[2].start()
    ay[3].wait_recv()
    ayr[3].start()
    aparts[qy, 0], aparts[qy, 1] = split(abuf[qy])
    start_relays(1)
    for copy in ayr:
        copy.wait_recv()
    aparts[qd, 0], aparts[qd, 1] = split(abuf[qd])

    def term(t, block):
        return dot3((aparts[block, 0], aparts[block, 1]), split(vbuf[block, t]))

    def image_of(t):
        total = term(t, p)
        for i in range(RELAYED, PIECES):
            vx[t][i].wait_recv()
        total += term(t, px)
        for i in range(RELAYED):
            vz[t][i].wait_recv()
        total += term(t, pz)
        for copy in (*vxr[t], *vzr[t]):
            copy.wait_recv()
        return split(total + term(t, pd))

    def send_partials(t, image):
        for j in range(0, CHUNKS, 2):
            span = pl.ds(j * chunk, 2 * chunk)
            block = dot3((left_t[1 - x, 0, span], left_t[1 - x, 1, span]), image)
            for k in range(2):
                csend[t, j + k] = block[k * chunk : (k + 1) * chunk]
                cx[t][j + k].start()

    def keep_partials(t, image):
        block = dot3((left_t[x, 0], left_t[x, 1]), image)
        for j in range(CHUNKS):
            cmine[t, j] = block[j * chunk : (j + 1) * chunk]

    swapped = slot_ref[w // GROUP_WIDE]
    same_flag = (((z + swapped + y) % 2) == 0).astype(jnp.int32)
    stays = core == y
    leaves = core != y

    def reduce_x(t, j):
        cx[t][j].wait_recv()
        total = cmine[t, j] + crecv[t, j]
        sums[t, j] = total

        @pl.when(leaves)
        def _():
            cross[t][j].start()

        @pl.when(stays & (core != t))
        def _():
            keep[t][j].start()

        @pl.when(stays & (core == t))
        def _():
            gsame[j] = total

    def select_z(t, j):
        @pl.when(core == t)
        def _():
            @pl.when(leaves)
            def _():
                keep[t][j].wait_recv()

            cross[t][j].wait_recv()
            same, other = gsame[j], gother[j]
            mask = jnp.full(same.shape, same_flag) == 1
            zsend[j] = jnp.where(mask, other, same)
            zc[j].start()
            o_ref[pl.ds(j * chunk, chunk), :] = jnp.where(mask, same, other)

    def finish(t, j):
        @pl.when(core == t)
        def _():
            zc[j].wait_recv()
            o_ref[pl.ds(j * chunk, chunk), :] += zrecv[j]

    image = image_of(0)
    send_partials(0, image)
    keep_partials(0, image)
    image = image_of(1)
    send_partials(1, image)
    keep_partials(1, image)

    steps = [(t, j) for t in range(2) for j in range(CHUNKS)]
    for step in range(len(steps) + 2):
        if step < len(steps):
            reduce_x(*steps[step])
        if 0 <= step - 1 < len(steps):
            select_z(*steps[step - 1])
        if 0 <= step - 2 < len(steps):
            finish(*steps[step - 2])

    flat = [copy for group in (*vx, *vz, *vxr, *vzr, *cx) for copy in group]
    for copy in (*flat, *ay, *ayr, vs, as_, *zc):
        copy.wait_send()
    for t in range(2):
        @pl.when(leaves)
        def _():
            for copy in cross[t]:
                copy.wait_send()

        @pl.when(stays & (core != t))
        def _():
            for copy in keep[t]:
                copy.wait_send()


def fast_body(moments, eigen_basis, slot_order):
    rows, cols = moments.shape
    f32 = jnp.float32
    chunk = rows // CHUNKS
    wide_half = cols // 2
    return pl.pallas_call(
        kernel,
        out_shape=jax.ShapeDtypeStruct((rows, wide_half), f32),
        in_specs=[
            pl.BlockSpec(memory_space=pltpu.SMEM),
            pl.BlockSpec(memory_space=pl.ANY),
            pl.BlockSpec(memory_space=pl.ANY),
        ],
        out_specs=pl.BlockSpec(memory_space=pltpu.VMEM),
        scratch_shapes=[
            pltpu.VMEM((4, rows, cols), f32),
            pltpu.VMEM((4, 2, rows, cols), jnp.bfloat16),
            pltpu.VMEM((4, 2, rows, wide_half), f32),
            pltpu.VMEM((2, rows, cols), f32),
            pltpu.VMEM((2, 2, cols, rows), jnp.bfloat16),
            *[pltpu.VMEM((2, CHUNKS, chunk, wide_half), f32)] * 4,
            *[pltpu.VMEM((CHUNKS, chunk, wide_half), f32)] * 4,
            pltpu.SemaphoreType.DMA((4,)),
            pltpu.SemaphoreType.DMA((COPIES,)),
            pltpu.SemaphoreType.DMA((COPIES,)),
        ],
        compiler_params=pltpu.CompilerParams(
            collective_id=0, has_side_effects=True, vmem_limit_bytes=56 * 1024 * 1024
        ),
        name="rayleigh",
    )(slot_order, moments, eigen_basis)


def partner(value, axis, stride):
    mask = 2**stride
    pairs = [(source, source ^ mask) for source in range(lax.axis_size(axis))]
    return lax.ppermute(value, axis, pairs)


def body(moments, eigen_basis, slot_order):
    wide_pos = lax.axis_index("wide")
    subproblem = wide_pos // GROUP_WIDE
    position = wide_pos % GROUP_WIDE
    swapped = lax.dynamic_index_in_dim(slot_order, subproblem, 0, keepdims=False)
    narrow_pos = lax.axis_index("narrow")
    col_count = eigen_basis.shape[1]
    half_cols = col_count // 2
    full_basis = lax.all_gather(eigen_basis, "narrow", axis=1, tiled=True)
    first_half = lax.dynamic_slice_in_dim(full_basis, narrow_pos * half_cols, half_cols, 1)
    second_half = lax.dynamic_slice_in_dim(full_basis, K + narrow_pos * half_cols, half_cols, 1)
    local_panel = jnp.concatenate([first_half, second_half], axis=1)
    pair_block = partner(local_panel, "wide", 0)
    joined = jnp.where(
        position % 2 == 0,
        jnp.concatenate([local_panel, pair_block], axis=0),
        jnp.concatenate([pair_block, local_panel], axis=0),
    )
    quad_block = partner(joined, "wide", 1)
    col_panel = jnp.where(
        position // 2 % 2 == 0,
        jnp.concatenate([joined, quad_block], axis=0),
        jnp.concatenate([quad_block, joined], axis=0),
    )
    products = jnp.dot(
        lax.all_gather(moments, "narrow", axis=1, tiled=True),
        col_panel,
        precision=lax.Precision.HIGHEST,
        preferred_element_type=jnp.float32,
    )
    partials = []
    for slot_index in range(2):
        half_panel = products[:, slot_index * half_cols : (slot_index + 1) * half_cols]
        vectors_half = full_basis[:, slot_index * K : (slot_index + 1) * K]
        partials.append(
            lax.dot_general(
                vectors_half,
                half_panel,
                (((0,), (0,)), ((), ())),
                precision=lax.Precision.HIGHEST,
                preferred_element_type=jnp.float32,
            )
        )
    stacked = jnp.stack(partials)
    slot_pick = (position // 2 + swapped) % 2
    row_part = position % 2
    summed = stacked + partner(stacked, "wide", 0)
    summed = summed + partner(summed, "wide", 1)
    chosen = lax.dynamic_index_in_dim(summed, slot_pick, 0, keepdims=False)
    return lax.dynamic_slice_in_dim(chosen, row_part * (K // 2), K // 2, 0)


def solution(mesh):
    placed = (P("wide", "narrow"), P("wide", "narrow"), P())
    cube = mesh.shape["narrow"] == 4
    return jax.shard_map(
        fast_body if cube else body, mesh=mesh, in_specs=placed, out_specs=P("wide", "narrow"), check_vma=False
    )
```

```python
import jax
import jax.numpy as jnp
from jax import lax
from jax.experimental import pallas as pl
from jax.experimental.pallas import tpu as pltpu
from jax.sharding import PartitionSpec as P

GROUP_WIDE = 4
K = 1024
MESH = pl.DeviceIdType.MESH
CHUNKS = 8
PIECES = 8
RELAYED = 5
LAG = 2
A_PIECES = 4
COPIES = 6 * PIECES + 2 * A_PIECES + 7 * CHUNKS + 2


def split(value):
    high = value.astype(jnp.bfloat16)
    low = (value - high.astype(jnp.float32)).astype(jnp.bfloat16)
    return high, low


def dot3(left, right):
    def dot(a, b):
        return jnp.dot(a, b, preferred_element_type=jnp.float32)

    return dot(left[0], right[0]) + (dot(left[0], right[1]) + dot(left[1], right[0]))


def kernel(
    slot_ref, a_ref, v_ref, o_ref,
    abuf, aparts, vbuf, left, left_t, csend, cmine, crecv, sums, gsame, gother, zsend, zrecv,
    local_sem, send_sem, recv_sem,
):
    rows, cols = a_ref.shape
    wide_half = cols // 2
    piece = rows // PIECES
    chunk = rows // CHUNKS
    w = lax.axis_index("wide")
    n = lax.axis_index("narrow")
    x = w % 2
    z = (w // 2) % 2
    y = n // 2
    core = n % 2
    p = w % 4
    wx = w + 1 - 2 * x
    wz = w + 2 - 4 * z
    px = p + 1 - 2 * x
    pz = p + 2 - 4 * z
    pd = 3 - p
    ns = n + 1 - 2 * core
    ny = n + 2 - 4 * y
    nd = 3 - n
    q = 2 * y + core
    qs = 2 * y + 1 - core
    qy = 2 * (1 - y) + core
    qd = 3 - q

    barrier = pltpu.get_barrier_semaphore()
    for target in ((wx, n), (wz, n), (w, ns), (w, ny), (w, nd)):
        pl.semaphore_signal(barrier, inc=1, device_id=target, device_id_type=MESH)

    def part(i):
        return pl.ds(i * piece, piece)

    def side(t):
        return pl.ds(t * wide_half, wide_half)

    local = [
        pltpu.make_async_copy(v_ref, left.at[core], local_sem.at[0]),
        pltpu.make_async_copy(a_ref, abuf.at[q], local_sem.at[1]),
        pltpu.make_async_copy(v_ref.at[:, side(0)], vbuf.at[p, 0], local_sem.at[2]),
        pltpu.make_async_copy(v_ref.at[:, side(1)], vbuf.at[p, 1], local_sem.at[3]),
    ]
    for copy in local:
        copy.start()

    used = []

    def remote(src, dst, target):
        index = len(used)
        used.append(index)
        return pltpu.make_async_remote_copy(
            src_ref=src, dst_ref=dst, send_sem=send_sem.at[index], recv_sem=recv_sem.at[index],
            device_id=target, device_id_type=MESH,
        )

    def own(t, i, target):
        return remote(v_ref.at[part(i), side(t)], vbuf.at[p, t, part(i)], target)

    def relay(t, i, block, target):
        return remote(vbuf.at[block, t, part(i)], vbuf.at[block, t, part(i)], target)

    vx = [[own(t, i, (wx, n)) for i in range(PIECES)] for t in range(2)]
    vz = [[own(t, i, (wz, n)) for i in range(PIECES)] for t in range(2)]
    vxr = [[relay(t, i, px, (wz, n)) for i in range(RELAYED)] for t in range(2)]
    vzr = [[relay(t, i, pz, (wx, n)) for i in range(RELAYED, PIECES)] for t in range(2)]
    a_rows = [pl.ds(i * (rows // A_PIECES), rows // A_PIECES) for i in range(A_PIECES)]
    ay = [remote(a_ref.at[span], abuf.at[q, span], (w, ny)) for span in a_rows]
    ayr = [remote(abuf.at[qy, span], abuf.at[qy, span], (w, ns)) for span in a_rows]
    vs = remote(v_ref, left.at[core], (w, ns))
    as_ = remote(a_ref, abuf.at[q], (w, ns))
    cx = [[remote(csend.at[t, j], crecv.at[t, j], (wx, n)) for j in range(CHUNKS)] for t in range(2)]
    keep = [[remote(sums.at[t, j], gsame.at[j], (w, ns)) for j in range(CHUNKS)] for t in range(2)]
    cross = [[remote(sums.at[t, j], gother.at[j], (w, 2 * (1 - y) + t)) for j in range(CHUNKS)] for t in range(2)]
    zc = [remote(zsend.at[j], zrecv.at[j], (wz, n)) for j in range(CHUNKS)]

    def start_own(t):
        for i in range(PIECES):
            vx[t][i].start()
            vz[t][PIECES - 1 - i].start()

    def start_relays(t):
        late = list(range(RELAYED, PIECES))[::-1]
        for i in range(max(RELAYED, PIECES - RELAYED)):
            if i < RELAYED:
                vx[t][i].wait_recv()
                vxr[t][i].start()
            if i < PIECES - RELAYED:
                vz[t][late[i]].wait_recv()
                vzr[t][late[i] - RELAYED].start()

    pl.semaphore_wait(barrier, 5)
    start_own(0)
    for copy in (*ay, vs, as_):
        copy.start()
    for copy in local:
        copy.wait()
    start_relays(0)
    start_own(1)
    ay[0].wait_recv()
    ayr[0].start()
    aparts[q, 0], aparts[q, 1] = split(abuf[q])
    left_t[core, 0], left_t[core, 1] = split(left[core].T)
    ay[1].wait_recv()
    ayr[1].start()
    vs.wait_recv()
    left_t[1 - core, 0], left_t[1 - core, 1] = split(left[1 - core].T)
    as_.wait_recv()
    aparts[qs, 0], aparts[qs, 1] = split(abuf[qs])
    ay[2].wait_recv()
    ayr[2].start()
    ay[3].wait_recv()
    ayr[3].start()
    aparts[qy, 0], aparts[qy, 1] = split(abuf[qy])
    start_relays(1)
    for copy in ayr:
        copy.wait_recv()
    aparts[qd, 0], aparts[qd, 1] = split(abuf[qd])

    def term(t, block):
        return dot3((aparts[block, 0], aparts[block, 1]), split(vbuf[block, t]))

    def image_of(t):
        total = term(t, p)
        for i in range(RELAYED, PIECES):
            vx[t][i].wait_recv()
        total += term(t, px)
        for i in range(RELAYED):
            vz[t][i].wait_recv()
        total += term(t, pz)
        for copy in (*vxr[t], *vzr[t]):
            copy.wait_recv()
        return split(total + term(t, pd))

    def send_partials(t, image):
        group = CHUNKS // 2
        for j in range(0, CHUNKS, group):
            span = pl.ds(j * chunk, group * chunk)
            block = dot3((left_t[1 - x, 0, span], left_t[1 - x, 1, span]), image)
            for k in range(group):
                csend[t, j + k] = block[k * chunk : (k + 1) * chunk]
                cx[t][j + k].start()

    def keep_partials(t, image):
        block = dot3((left_t[x, 0], left_t[x, 1]), image)
        for j in range(CHUNKS):
            cmine[t, j] = block[j * chunk : (j + 1) * chunk]

    swapped = slot_ref[w // GROUP_WIDE]
    same_flag = (((z + swapped + y) % 2) == 0).astype(jnp.int32)
    stays = core == y
    leaves = core != y

    def reduce_x(t, j):
        cx[t][j].wait_recv()
        total = cmine[t, j] + crecv[t, j]
        sums[t, j] = total

        @pl.when(leaves)
        def _():
            cross[t][j].start()

        @pl.when(stays & (core != t))
        def _():
            keep[t][j].start()

        @pl.when(stays & (core == t))
        def _():
            gsame[j] = total

    def select_z(t, j):
        @pl.when(core == t)
        def _():
            @pl.when(leaves)
            def _():
                keep[t][j].wait_recv()

            cross[t][j].wait_recv()
            same, other = gsame[j], gother[j]
            mask = jnp.full(same.shape, same_flag) == 1
            zsend[j] = jnp.where(mask, other, same)
            zc[j].start()
            o_ref[pl.ds(j * chunk, chunk), :] = jnp.where(mask, same, other)

    def finish(t, j):
        @pl.when(core == t)
        def _():
            zc[j].wait_recv()
            o_ref[pl.ds(j * chunk, chunk), :] += zrecv[j]

    image = image_of(0)
    send_partials(0, image)
    keep_partials(0, image)
    image = image_of(1)
    send_partials(1, image)
    keep_partials(1, image)

    for j in range(CHUNKS):
        reduce_x(0, j)
    for j in range(CHUNKS):
        select_z(0, j)
    for j in range(CHUNKS + LAG):
        if j < CHUNKS:
            reduce_x(1, j)
        if j >= LAG:
            select_z(1, j - LAG)
    for t in range(2):
        for j in range(CHUNKS):
            finish(t, j)

    flat = [copy for group in (*vx, *vz, *vxr, *vzr, *cx) for copy in group]
    for copy in (*flat, *ay, *ayr, vs, as_, *zc):
        copy.wait_send()
    for t in range(2):
        @pl.when(leaves)
        def _():
            for copy in cross[t]:
                copy.wait_send()

        @pl.when(stays & (core != t))
        def _():
            for copy in keep[t]:
                copy.wait_send()


def fast_body(moments, eigen_basis, slot_order):
    rows, cols = moments.shape
    f32 = jnp.float32
    chunk = rows // CHUNKS
    wide_half = cols // 2
    return pl.pallas_call(
        kernel,
        out_shape=jax.ShapeDtypeStruct((rows, wide_half), f32),
        in_specs=[
            pl.BlockSpec(memory_space=pltpu.SMEM),
            pl.BlockSpec(memory_space=pl.ANY),
            pl.BlockSpec(memory_space=pl.ANY),
        ],
        out_specs=pl.BlockSpec(memory_space=pltpu.VMEM),
        scratch_shapes=[
            pltpu.VMEM((4, rows, cols), f32),
            pltpu.VMEM((4, 2, rows, cols), jnp.bfloat16),
            pltpu.VMEM((4, 2, rows, wide_half), f32),
            pltpu.VMEM((2, rows, cols), f32),
            pltpu.VMEM((2, 2, cols, rows), jnp.bfloat16),
            *[pltpu.VMEM((2, CHUNKS, chunk, wide_half), f32)] * 4,
            *[pltpu.VMEM((CHUNKS, chunk, wide_half), f32)] * 4,
            pltpu.SemaphoreType.DMA((4,)),
            pltpu.SemaphoreType.DMA((COPIES,)),
            pltpu.SemaphoreType.DMA((COPIES,)),
        ],
        compiler_params=pltpu.CompilerParams(
            collective_id=0, has_side_effects=True, vmem_limit_bytes=56 * 1024 * 1024
        ),
        name="rayleigh",
    )(slot_order, moments, eigen_basis)


def partner(value, axis, stride):
    mask = 2**stride
    pairs = [(source, source ^ mask) for source in range(lax.axis_size(axis))]
    return lax.ppermute(value, axis, pairs)


def body(moments, eigen_basis, slot_order):
    wide_pos = lax.axis_index("wide")
    subproblem = wide_pos // GROUP_WIDE
    position = wide_pos % GROUP_WIDE
    swapped = lax.dynamic_index_in_dim(slot_order, subproblem, 0, keepdims=False)
    narrow_pos = lax.axis_index("narrow")
    col_count = eigen_basis.shape[1]
    half_cols = col_count // 2
    full_basis = lax.all_gather(eigen_basis, "narrow", axis=1, tiled=True)
    first_half = lax.dynamic_slice_in_dim(full_basis, narrow_pos * half_cols, half_cols, 1)
    second_half = lax.dynamic_slice_in_dim(full_basis, K + narrow_pos * half_cols, half_cols, 1)
    local_panel = jnp.concatenate([first_half, second_half], axis=1)
    pair_block = partner(local_panel, "wide", 0)
    joined = jnp.where(
        position % 2 == 0,
        jnp.concatenate([local_panel, pair_block], axis=0),
        jnp.concatenate([pair_block, local_panel], axis=0),
    )
    quad_block = partner(joined, "wide", 1)
    col_panel = jnp.where(
        position // 2 % 2 == 0,
        jnp.concatenate([joined, quad_block], axis=0),
        jnp.concatenate([quad_block, joined], axis=0),
    )
    products = jnp.dot(
        lax.all_gather(moments, "narrow", axis=1, tiled=True),
        col_panel,
        precision=lax.Precision.HIGHEST,
        preferred_element_type=jnp.float32,
    )
    partials = []
    for slot_index in range(2):
        half_panel = products[:, slot_index * half_cols : (slot_index + 1) * half_cols]
        vectors_half = full_basis[:, slot_index * K : (slot_index + 1) * K]
        partials.append(
            lax.dot_general(
                vectors_half,
                half_panel,
                (((0,), (0,)), ((), ())),
                precision=lax.Precision.HIGHEST,
                preferred_element_type=jnp.float32,
            )
        )
    stacked = jnp.stack(partials)
    slot_pick = (position // 2 + swapped) % 2
    row_part = position % 2
    summed = stacked + partner(stacked, "wide", 0)
    summed = summed + partner(summed, "wide", 1)
    chosen = lax.dynamic_index_in_dim(summed, slot_pick, 0, keepdims=False)
    return lax.dynamic_slice_in_dim(chosen, row_part * (K // 2), K // 2, 0)


def solution(mesh):
    placed = (P("wide", "narrow"), P("wide", "narrow"), P())
    cube = mesh.shape["narrow"] == 4
    return jax.shard_map(
        fast_body if cube else body, mesh=mesh, in_specs=placed, out_specs=P("wide", "narrow"), check_vma=False
    )
```

```python
import jax
import jax.numpy as jnp
from jax import lax
from jax.experimental import pallas as pl
from jax.experimental.pallas import tpu as pltpu
from jax.sharding import PartitionSpec as P

GROUP_WIDE = 4
K = 1024
MESH = pl.DeviceIdType.MESH
CHUNKS = 8
PIECES = 8
RELAYED = 5
LAG = 1
SPLIT = 3
DIRECT = CHUNKS - SPLIT
A_PIECES = 4
COPIES = 6 * PIECES + 2 * A_PIECES + 7 * CHUNKS + 2 + 3 * SPLIT


def split(value):
    high = value.astype(jnp.bfloat16)
    low = (value - high.astype(jnp.float32)).astype(jnp.bfloat16)
    return high, low


def dot3(left, right):
    def dot(a, b):
        return jnp.dot(a, b, preferred_element_type=jnp.float32)

    return dot(left[0], right[0]) + (dot(left[0], right[1]) + dot(left[1], right[0]))


def kernel(
    slot_ref, a_ref, v_ref, o_ref,
    abuf, aparts, vbuf, left, left_t, csend, cmine, crecv, sums, gsame, gother, zsend, zrecv,
    fpart, frecv, fsend, fback, fsums, fsame, fother, fzsend, fzrecv,
    local_sem, send_sem, recv_sem,
):
    rows, cols = a_ref.shape
    wide_half = cols // 2
    piece = rows // PIECES
    chunk = rows // CHUNKS
    sub = chunk // 2
    w = lax.axis_index("wide")
    n = lax.axis_index("narrow")
    x = w % 2
    z = (w // 2) % 2
    y = n // 2
    core = n % 2
    p = w % 4
    wx = w + 1 - 2 * x
    wz = w + 2 - 4 * z
    px = p + 1 - 2 * x
    pz = p + 2 - 4 * z
    pd = 3 - p
    ns = n + 1 - 2 * core
    ny = n + 2 - 4 * y
    nd = 3 - n
    q = 2 * y + core
    qs = 2 * y + 1 - core
    qy = 2 * (1 - y) + core
    qd = 3 - q

    barrier = pltpu.get_barrier_semaphore()
    for target in ((wx, n), (wz, n), (w, ns), (w, ny), (w, nd)):
        pl.semaphore_signal(barrier, inc=1, device_id=target, device_id_type=MESH)

    def part(i):
        return pl.ds(i * piece, piece)

    def side(t):
        return pl.ds(t * wide_half, wide_half)

    local = [
        pltpu.make_async_copy(v_ref, left.at[core], local_sem.at[0]),
        pltpu.make_async_copy(a_ref, abuf.at[q], local_sem.at[1]),
        pltpu.make_async_copy(v_ref.at[:, side(0)], vbuf.at[p, 0], local_sem.at[2]),
        pltpu.make_async_copy(v_ref.at[:, side(1)], vbuf.at[p, 1], local_sem.at[3]),
    ]
    for copy in local:
        copy.start()

    used = []

    def remote(src, dst, target):
        index = len(used)
        used.append(index)
        return pltpu.make_async_remote_copy(
            src_ref=src, dst_ref=dst, send_sem=send_sem.at[index], recv_sem=recv_sem.at[index],
            device_id=target, device_id_type=MESH,
        )

    def own(t, i, target):
        return remote(v_ref.at[part(i), side(t)], vbuf.at[p, t, part(i)], target)

    def relay(t, i, block, target):
        return remote(vbuf.at[block, t, part(i)], vbuf.at[block, t, part(i)], target)

    vx = [[own(t, i, (wx, n)) for i in range(PIECES)] for t in range(2)]
    vz = [[own(t, i, (wz, n)) for i in range(PIECES)] for t in range(2)]
    vxr = [[relay(t, i, px, (wz, n)) for i in range(RELAYED)] for t in range(2)]
    vzr = [[relay(t, i, pz, (wx, n)) for i in range(RELAYED, PIECES)] for t in range(2)]
    a_rows = [pl.ds(i * (rows // A_PIECES), rows // A_PIECES) for i in range(A_PIECES)]
    ay = [remote(a_ref.at[span], abuf.at[q, span], (w, ny)) for span in a_rows]
    ayr = [remote(abuf.at[qy, span], abuf.at[qy, span], (w, ns)) for span in a_rows]
    vs = remote(v_ref, left.at[core], (w, ns))
    as_ = remote(a_ref, abuf.at[q], (w, ns))
    cx = [[remote(csend.at[t, j], crecv.at[t, j], (wx, n)) for j in range(count)] for t, count in enumerate((CHUNKS, DIRECT))]
    keep = [[remote(sums.at[t, j], gsame.at[j], (w, ns)) for j in range(count)] for t, count in enumerate((CHUNKS, DIRECT))]
    cross = [[remote(sums.at[t, j], gother.at[j], (w, 2 * (1 - y) + t)) for j in range(count)] for t, count in enumerate((CHUNKS, DIRECT))]
    zc = [remote(zsend.at[j], zrecv.at[j], (wz, n)) for j in range(CHUNKS)]
    mine_rows = pl.ds(pl.multiple_of(z * sub, sub), sub)
    theirs_rows = pl.ds(pl.multiple_of((1 - z) * sub, sub), sub)
    zf = [[remote(fpart.at[i, a, theirs_rows], frecv.at[i, a], (wz, n)) for a in range(2)] for i in range(SPLIT)]
    xf = [remote(fsend.at[i], fback.at[i], (wx, n)) for i in range(SPLIT)]
    keepf = [remote(fsums.at[i], fsame.at[i], (w, ns)) for i in range(SPLIT)]
    crossf = [remote(fsums.at[i], fother.at[i], (w, 2 * (1 - y) + 1)) for i in range(SPLIT)]
    zf2 = [remote(fzsend.at[i], fzrecv.at[i], (wz, n)) for i in range(SPLIT)]

    def start_own(t):
        for i in range(PIECES):
            vx[t][i].start()
            vz[t][PIECES - 1 - i].start()

    def start_relays(t):
        late = list(range(RELAYED, PIECES))[::-1]
        for i in range(max(RELAYED, PIECES - RELAYED)):
            if i < RELAYED:
                vx[t][i].wait_recv()
                vxr[t][i].start()
            if i < PIECES - RELAYED:
                vz[t][late[i]].wait_recv()
                vzr[t][late[i] - RELAYED].start()

    pl.semaphore_wait(barrier, 5)
    start_own(0)
    for copy in (*ay, vs, as_):
        copy.start()
    for copy in local:
        copy.wait()
    start_relays(0)
    start_own(1)
    ay[0].wait_recv()
    ayr[0].start()
    aparts[q, 0], aparts[q, 1] = split(abuf[q])
    left_t[core, 0], left_t[core, 1] = split(left[core].T)
    ay[1].wait_recv()
    ayr[1].start()
    vs.wait_recv()
    left_t[1 - core, 0], left_t[1 - core, 1] = split(left[1 - core].T)
    as_.wait_recv()
    aparts[qs, 0], aparts[qs, 1] = split(abuf[qs])
    ay[2].wait_recv()
    ayr[2].start()
    ay[3].wait_recv()
    ayr[3].start()
    aparts[qy, 0], aparts[qy, 1] = split(abuf[qy])
    start_relays(1)
    for copy in ayr:
        copy.wait_recv()
    aparts[qd, 0], aparts[qd, 1] = split(abuf[qd])

    def term(t, block):
        return dot3((aparts[block, 0], aparts[block, 1]), split(vbuf[block, t]))

    def image_of(t):
        total = term(t, p)
        for i in range(RELAYED, PIECES):
            vx[t][i].wait_recv()
        total += term(t, px)
        for i in range(RELAYED):
            vz[t][i].wait_recv()
        total += term(t, pz)
        for copy in (*vxr[t], *vzr[t]):
            copy.wait_recv()
        return split(total + term(t, pd))

    def send_partials(t, image):
        group = CHUNKS // 2
        for j in range(0, CHUNKS, group):
            span = pl.ds(j * chunk, group * chunk)
            block = dot3((left_t[1 - x, 0, span], left_t[1 - x, 1, span]), image)
            for k in range(group):
                value = block[k * chunk : (k + 1) * chunk]
                if j + k < len(cx[t]):
                    csend[t, j + k] = value
                    cx[t][j + k].start()
                else:
                    fpart[j + k - DIRECT, 0] = value
                    zf[j + k - DIRECT][0].start()

    def keep_partials(t, image):
        block = dot3((left_t[x, 0], left_t[x, 1]), image)
        for j in range(CHUNKS):
            value = block[j * chunk : (j + 1) * chunk]
            if j < len(cx[t]):
                cmine[t, j] = value
            else:
                fpart[j - DIRECT, 1] = value
                zf[j - DIRECT][1].start()

    swapped = slot_ref[w // GROUP_WIDE]
    same_flag = (((z + swapped + y) % 2) == 0).astype(jnp.int32)
    stays = core == y
    leaves = core != y

    def reduce_x(t, j):
        cx[t][j].wait_recv()
        total = cmine[t, j] + crecv[t, j]
        sums[t, j] = total

        @pl.when(leaves)
        def _():
            cross[t][j].start()

        @pl.when(stays & (core != t))
        def _():
            keep[t][j].start()

        @pl.when(stays & (core == t))
        def _():
            gsame[j] = total

    def select_z(t, j):
        @pl.when(core == t)
        def _():
            @pl.when(leaves)
            def _():
                keep[t][j].wait_recv()

            cross[t][j].wait_recv()
            same, other = gsame[j], gother[j]
            mask = jnp.full(same.shape, same_flag) == 1
            zsend[j] = jnp.where(mask, other, same)
            zc[j].start()
            o_ref[pl.ds(j * chunk, chunk), :] = jnp.where(mask, same, other)

    def finish(t, j):
        @pl.when(core == t)
        def _():
            zc[j].wait_recv()
            o_ref[pl.ds(j * chunk, chunk), :] += zrecv[j]

    def split_x(i):
        zf[i][0].wait_recv()
        fsend[i] = fpart[i, 0, mine_rows] + frecv[i, 0]
        xf[i].start()

    def split_y(i):
        zf[i][1].wait_recv()
        xf[i].wait_recv()
        total = fpart[i, 1, mine_rows] + frecv[i, 1] + fback[i]
        fsums[i] = total

        @pl.when(leaves)
        def _():
            crossf[i].start()

        @pl.when(stays & (core == 0))
        def _():
            keepf[i].start()

        @pl.when(stays & (core == 1))
        def _():
            fsame[i] = total

    def split_z(i):
        @pl.when(core == 1)
        def _():
            @pl.when(leaves)
            def _():
                keepf[i].wait_recv()

            crossf[i].wait_recv()
            same, other = fsame[i], fother[i]
            mask = jnp.full(same.shape, same_flag) == 1
            fzsend[i] = jnp.where(mask, other, same)
            zf2[i].start()
            base = (DIRECT + i) * chunk + z * sub
            o_ref[pl.ds(pl.multiple_of(base, sub), sub), :] = jnp.where(mask, same, other)

    def split_finish(i):
        @pl.when(core == 1)
        def _():
            zf2[i].wait_recv()
            base = (DIRECT + i) * chunk + (1 - z) * sub
            o_ref[pl.ds(pl.multiple_of(base, sub), sub), :] = fzrecv[i]

    image = image_of(0)
    send_partials(0, image)
    keep_partials(0, image)
    image = image_of(1)
    send_partials(1, image)
    keep_partials(1, image)

    for j in range(CHUNKS):
        reduce_x(0, j)
    for j in range(CHUNKS):
        select_z(0, j)
    for i in range(SPLIT):
        split_x(i)
    for j in range(DIRECT):
        reduce_x(1, j)
        if j >= LAG:
            select_z(1, j - LAG)
    for i in range(SPLIT):
        split_y(i)
        if i < LAG:
            select_z(1, DIRECT - LAG + i)
        else:
            split_z(i - LAG)
    for i in range(SPLIT - LAG, SPLIT):
        split_z(i)
    for j in range(CHUNKS):
        finish(0, j)
    for j in range(DIRECT):
        finish(1, j)
    for i in range(SPLIT):
        split_finish(i)

    flat = [copy for group in (*vx, *vz, *vxr, *vzr, *cx, *zf) for copy in group]
    for copy in (*flat, *ay, *ayr, vs, as_, *xf, *zc[:DIRECT]):
        copy.wait_send()

    @pl.when(core == 0)
    def _():
        for copy in zc[DIRECT:]:
            copy.wait_send()

    @pl.when(core == 1)
    def _():
        for copy in zf2:
            copy.wait_send()

    @pl.when(leaves)
    def _():
        for copy in crossf:
            copy.wait_send()

    @pl.when(stays & (core == 0))
    def _():
        for copy in keepf:
            copy.wait_send()

    for t in range(2):
        @pl.when(leaves)
        def _():
            for copy in cross[t]:
                copy.wait_send()

        @pl.when(stays & (core != t))
        def _():
            for copy in keep[t]:
                copy.wait_send()


def fast_body(moments, eigen_basis, slot_order):
    rows, cols = moments.shape
    f32 = jnp.float32
    chunk = rows // CHUNKS
    wide_half = cols // 2
    return pl.pallas_call(
        kernel,
        out_shape=jax.ShapeDtypeStruct((rows, wide_half), f32),
        in_specs=[
            pl.BlockSpec(memory_space=pltpu.SMEM),
            pl.BlockSpec(memory_space=pl.ANY),
            pl.BlockSpec(memory_space=pl.ANY),
        ],
        out_specs=pl.BlockSpec(memory_space=pltpu.VMEM),
        scratch_shapes=[
            pltpu.VMEM((4, rows, cols), f32),
            pltpu.VMEM((4, 2, rows, cols), jnp.bfloat16),
            pltpu.VMEM((4, 2, rows, wide_half), f32),
            pltpu.VMEM((2, rows, cols), f32),
            pltpu.VMEM((2, 2, cols, rows), jnp.bfloat16),
            *[pltpu.VMEM((2, CHUNKS, chunk, wide_half), f32)] * 4,
            *[pltpu.VMEM((CHUNKS, chunk, wide_half), f32)] * 4,
            pltpu.VMEM((SPLIT, 2, chunk, wide_half), f32),
            pltpu.VMEM((SPLIT, 2, chunk // 2, wide_half), f32),
            *[pltpu.VMEM((SPLIT, chunk // 2, wide_half), f32)] * 7,
            pltpu.SemaphoreType.DMA((4,)),
            pltpu.SemaphoreType.DMA((COPIES,)),
            pltpu.SemaphoreType.DMA((COPIES,)),
        ],
        compiler_params=pltpu.CompilerParams(
            collective_id=0, has_side_effects=True, vmem_limit_bytes=56 * 1024 * 1024
        ),
        name="rayleigh",
    )(slot_order, moments, eigen_basis)


def partner(value, axis, stride):
    mask = 2**stride
    pairs = [(source, source ^ mask) for source in range(lax.axis_size(axis))]
    return lax.ppermute(value, axis, pairs)


def body(moments, eigen_basis, slot_order):
    wide_pos = lax.axis_index("wide")
    subproblem = wide_pos // GROUP_WIDE
    position = wide_pos % GROUP_WIDE
    swapped = lax.dynamic_index_in_dim(slot_order, subproblem, 0, keepdims=False)
    narrow_pos = lax.axis_index("narrow")
    col_count = eigen_basis.shape[1]
    half_cols = col_count // 2
    full_basis = lax.all_gather(eigen_basis, "narrow", axis=1, tiled=True)
    first_half = lax.dynamic_slice_in_dim(full_basis, narrow_pos * half_cols, half_cols, 1)
    second_half = lax.dynamic_slice_in_dim(full_basis, K + narrow_pos * half_cols, half_cols, 1)
    local_panel = jnp.concatenate([first_half, second_half], axis=1)
    pair_block = partner(local_panel, "wide", 0)
    joined = jnp.where(
        position % 2 == 0,
        jnp.concatenate([local_panel, pair_block], axis=0),
        jnp.concatenate([pair_block, local_panel], axis=0),
    )
    quad_block = partner(joined, "wide", 1)
    col_panel = jnp.where(
        position // 2 % 2 == 0,
        jnp.concatenate([joined, quad_block], axis=0),
        jnp.concatenate([quad_block, joined], axis=0),
    )
    products = jnp.dot(
        lax.all_gather(moments, "narrow", axis=1, tiled=True),
        col_panel,
        precision=lax.Precision.HIGHEST,
        preferred_element_type=jnp.float32,
    )
    partials = []
    for slot_index in range(2):
        half_panel = products[:, slot_index * half_cols : (slot_index + 1) * half_cols]
        vectors_half = full_basis[:, slot_index * K : (slot_index + 1) * K]
        partials.append(
            lax.dot_general(
                vectors_half,
                half_panel,
                (((0,), (0,)), ((), ())),
                precision=lax.Precision.HIGHEST,
                preferred_element_type=jnp.float32,
            )
        )
    stacked = jnp.stack(partials)
    slot_pick = (position // 2 + swapped) % 2
    row_part = position % 2
    summed = stacked + partner(stacked, "wide", 0)
    summed = summed + partner(summed, "wide", 1)
    chosen = lax.dynamic_index_in_dim(summed, slot_pick, 0, keepdims=False)
    return lax.dynamic_slice_in_dim(chosen, row_part * (K // 2), K // 2, 0)


def solution(mesh):
    placed = (P("wide", "narrow"), P("wide", "narrow"), P())
    cube = mesh.shape["narrow"] == 4
    return jax.shard_map(
        fast_body if cube else body, mesh=mesh, in_specs=placed, out_specs=P("wide", "narrow"), check_vma=False
    )
```

```python
import jax
import jax.numpy as jnp
from jax import lax
from jax.experimental import pallas as pl
from jax.experimental.pallas import tpu as pltpu
from jax.sharding import PartitionSpec as P

GROUP_WIDE = 4
K = 1024
MESH = pl.DeviceIdType.MESH
CHUNKS = 8
PIECES = 8
RELAYED = 5
LAG = 1
SPLIT = 4
DIRECT = CHUNKS - SPLIT
A_PIECES = 4
COPIES = 6 * PIECES + 2 * A_PIECES + 7 * CHUNKS + 2 + 3 * SPLIT


def split(value):
    high = value.astype(jnp.bfloat16)
    low = (value - high.astype(jnp.float32)).astype(jnp.bfloat16)
    return high, low


def dot3(left, right):
    def dot(a, b):
        return jnp.dot(a, b, preferred_element_type=jnp.float32)

    return dot(left[0], right[0]) + (dot(left[0], right[1]) + dot(left[1], right[0]))


def kernel(
    slot_ref, a_ref, v_ref, o_ref,
    abuf, aparts, vbuf, left, left_t, csend, cmine, crecv, sums, gsame, gother, zsend, zrecv,
    fpart, frecv, fsend, fback, fsums, fsame, fother, fzsend, fzrecv,
    local_sem, send_sem, recv_sem,
):
    rows, cols = a_ref.shape
    wide_half = cols // 2
    piece = rows // PIECES
    chunk = rows // CHUNKS
    sub = chunk // 2
    w = lax.axis_index("wide")
    n = lax.axis_index("narrow")
    x = w % 2
    z = (w // 2) % 2
    y = n // 2
    core = n % 2
    p = w % 4
    wx = w + 1 - 2 * x
    wz = w + 2 - 4 * z
    px = p + 1 - 2 * x
    pz = p + 2 - 4 * z
    pd = 3 - p
    ns = n + 1 - 2 * core
    ny = n + 2 - 4 * y
    nd = 3 - n
    q = 2 * y + core
    qs = 2 * y + 1 - core
    qy = 2 * (1 - y) + core
    qd = 3 - q

    barrier = pltpu.get_barrier_semaphore()
    for target in ((wx, n), (wz, n), (w, ns), (w, ny), (w, nd)):
        pl.semaphore_signal(barrier, inc=1, device_id=target, device_id_type=MESH)

    def part(i):
        return pl.ds(i * piece, piece)

    def side(t):
        return pl.ds(t * wide_half, wide_half)

    local = [
        pltpu.make_async_copy(v_ref, left.at[core], local_sem.at[0]),
        pltpu.make_async_copy(a_ref, abuf.at[q], local_sem.at[1]),
        pltpu.make_async_copy(v_ref.at[:, side(0)], vbuf.at[p, 0], local_sem.at[2]),
        pltpu.make_async_copy(v_ref.at[:, side(1)], vbuf.at[p, 1], local_sem.at[3]),
    ]
    for copy in local:
        copy.start()

    used = []

    def remote(src, dst, target):
        index = len(used)
        used.append(index)
        return pltpu.make_async_remote_copy(
            src_ref=src, dst_ref=dst, send_sem=send_sem.at[index], recv_sem=recv_sem.at[index],
            device_id=target, device_id_type=MESH,
        )

    def own(t, i, target):
        return remote(v_ref.at[part(i), side(t)], vbuf.at[p, t, part(i)], target)

    def relay(t, i, block, target):
        return remote(vbuf.at[block, t, part(i)], vbuf.at[block, t, part(i)], target)

    vx = [[own(t, i, (wx, n)) for i in range(PIECES)] for t in range(2)]
    vz = [[own(t, i, (wz, n)) for i in range(PIECES)] for t in range(2)]
    vxr = [[relay(t, i, px, (wz, n)) for i in range(RELAYED)] for t in range(2)]
    vzr = [[relay(t, i, pz, (wx, n)) for i in range(RELAYED, PIECES)] for t in range(2)]
    a_rows = [pl.ds(i * (rows // A_PIECES), rows // A_PIECES) for i in range(A_PIECES)]
    ay = [remote(a_ref.at[span], abuf.at[q, span], (w, ny)) for span in a_rows]
    ayr = [remote(abuf.at[qy, span], abuf.at[qy, span], (w, ns)) for span in a_rows]
    vs = remote(v_ref, left.at[core], (w, ns))
    as_ = remote(a_ref, abuf.at[q], (w, ns))
    cx = [[remote(csend.at[t, j], crecv.at[t, j], (wx, n)) for j in range(count)] for t, count in enumerate((CHUNKS, DIRECT))]
    keep = [[remote(sums.at[t, j], gsame.at[j], (w, ns)) for j in range(count)] for t, count in enumerate((CHUNKS, DIRECT))]
    cross = [[remote(sums.at[t, j], gother.at[j], (w, 2 * (1 - y) + t)) for j in range(count)] for t, count in enumerate((CHUNKS, DIRECT))]
    zc = [remote(zsend.at[j], zrecv.at[j], (wz, n)) for j in range(CHUNKS)]
    mine_rows = pl.ds(pl.multiple_of(z * sub, sub), sub)
    theirs_rows = pl.ds(pl.multiple_of((1 - z) * sub, sub), sub)
    zf = [[remote(fpart.at[i, a, theirs_rows], frecv.at[i, a], (wz, n)) for a in range(2)] for i in range(SPLIT)]
    xf = [remote(fsend.at[i], fback.at[i], (wx, n)) for i in range(SPLIT)]
    keepf = [remote(fsums.at[i], fsame.at[i], (w, ns)) for i in range(SPLIT)]
    crossf = [remote(fsums.at[i], fother.at[i], (w, 2 * (1 - y) + 1)) for i in range(SPLIT)]
    zf2 = [remote(fzsend.at[i], fzrecv.at[i], (wz, n)) for i in range(SPLIT)]

    def start_own(t):
        for i in range(PIECES):
            vx[t][i].start()
            vz[t][PIECES - 1 - i].start()

    def start_relays(t):
        late = list(range(RELAYED, PIECES))[::-1]
        for i in range(max(RELAYED, PIECES - RELAYED)):
            if i < RELAYED:
                vx[t][i].wait_recv()
                vxr[t][i].start()
            if i < PIECES - RELAYED:
                vz[t][late[i]].wait_recv()
                vzr[t][late[i] - RELAYED].start()

    pl.semaphore_wait(barrier, 5)
    start_own(0)
    for copy in (*ay, vs, as_):
        copy.start()
    for copy in local:
        copy.wait()
    start_relays(0)
    start_own(1)
    ay[0].wait_recv()
    ayr[0].start()
    aparts[q, 0], aparts[q, 1] = split(abuf[q])
    left_t[core, 0], left_t[core, 1] = split(left[core].T)
    ay[1].wait_recv()
    ayr[1].start()
    vs.wait_recv()
    left_t[1 - core, 0], left_t[1 - core, 1] = split(left[1 - core].T)
    as_.wait_recv()
    aparts[qs, 0], aparts[qs, 1] = split(abuf[qs])
    ay[2].wait_recv()
    ayr[2].start()
    ay[3].wait_recv()
    ayr[3].start()
    aparts[qy, 0], aparts[qy, 1] = split(abuf[qy])
    start_relays(1)
    for copy in ayr:
        copy.wait_recv()
    aparts[qd, 0], aparts[qd, 1] = split(abuf[qd])

    def term(t, block):
        return dot3((aparts[block, 0], aparts[block, 1]), split(vbuf[block, t]))

    def image_of(t):
        total = term(t, p)
        for i in range(RELAYED, PIECES):
            vx[t][i].wait_recv()
        total += term(t, px)
        for i in range(RELAYED):
            vz[t][i].wait_recv()
        total += term(t, pz)
        for copy in (*vxr[t], *vzr[t]):
            copy.wait_recv()
        return split(total + term(t, pd))

    def send_partials(t, image):
        group = CHUNKS // 2
        for j in range(0, CHUNKS, group):
            span = pl.ds(j * chunk, group * chunk)
            block = dot3((left_t[1 - x, 0, span], left_t[1 - x, 1, span]), image)
            for k in range(group):
                value = block[k * chunk : (k + 1) * chunk]
                if j + k < len(cx[t]):
                    csend[t, j + k] = value
                    cx[t][j + k].start()
                else:
                    fpart[j + k - DIRECT, 0] = value
                    zf[j + k - DIRECT][0].start()

    def keep_partials(t, image):
        block = dot3((left_t[x, 0], left_t[x, 1]), image)
        for j in range(CHUNKS):
            value = block[j * chunk : (j + 1) * chunk]
            if j < len(cx[t]):
                cmine[t, j] = value
            else:
                fpart[j - DIRECT, 1] = value
                zf[j - DIRECT][1].start()

    swapped = slot_ref[w // GROUP_WIDE]
    same_flag = (((z + swapped + y) % 2) == 0).astype(jnp.int32)
    stays = core == y
    leaves = core != y

    def reduce_x(t, j):
        cx[t][j].wait_recv()
        total = cmine[t, j] + crecv[t, j]
        sums[t, j] = total

        @pl.when(leaves)
        def _():
            cross[t][j].start()

        @pl.when(stays & (core != t))
        def _():
            keep[t][j].start()

        @pl.when(stays & (core == t))
        def _():
            gsame[j] = total

    def select_z(t, j):
        @pl.when(core == t)
        def _():
            @pl.when(leaves)
            def _():
                keep[t][j].wait_recv()

            cross[t][j].wait_recv()
            same, other = gsame[j], gother[j]
            mask = jnp.full(same.shape, same_flag) == 1
            zsend[j] = jnp.where(mask, other, same)
            zc[j].start()
            o_ref[pl.ds(j * chunk, chunk), :] = jnp.where(mask, same, other)

    def finish(t, j):
        @pl.when(core == t)
        def _():
            zc[j].wait_recv()
            o_ref[pl.ds(j * chunk, chunk), :] += zrecv[j]

    def split_x(i):
        zf[i][0].wait_recv()
        fsend[i] = fpart[i, 0, mine_rows] + frecv[i, 0]
        xf[i].start()

    def split_y(i):
        zf[i][1].wait_recv()
        xf[i].wait_recv()
        total = fpart[i, 1, mine_rows] + frecv[i, 1] + fback[i]
        fsums[i] = total

        @pl.when(leaves)
        def _():
            crossf[i].start()

        @pl.when(stays & (core == 0))
        def _():
            keepf[i].start()

        @pl.when(stays & (core == 1))
        def _():
            fsame[i] = total

    def split_z(i):
        @pl.when(core == 1)
        def _():
            @pl.when(leaves)
            def _():
                keepf[i].wait_recv()

            crossf[i].wait_recv()
            same, other = fsame[i], fother[i]
            mask = jnp.full(same.shape, same_flag) == 1
            fzsend[i] = jnp.where(mask, other, same)
            zf2[i].start()
            base = (DIRECT + i) * chunk + z * sub
            o_ref[pl.ds(pl.multiple_of(base, sub), sub), :] = jnp.where(mask, same, other)

    def split_finish(i):
        @pl.when(core == 1)
        def _():
            zf2[i].wait_recv()
            base = (DIRECT + i) * chunk + (1 - z) * sub
            o_ref[pl.ds(pl.multiple_of(base, sub), sub), :] = fzrecv[i]

    image = image_of(0)
    send_partials(0, image)
    keep_partials(0, image)
    image = image_of(1)
    send_partials(1, image)
    keep_partials(1, image)

    for j in range(CHUNKS):
        reduce_x(0, j)
    for j in range(CHUNKS):
        select_z(0, j)
    for i in range(SPLIT):
        split_x(i)
    for j in range(DIRECT):
        reduce_x(1, j)
        if j >= LAG:
            select_z(1, j - LAG)
    for i in range(SPLIT):
        split_y(i)
        if i < LAG:
            select_z(1, DIRECT - LAG + i)
        else:
            split_z(i - LAG)
    for i in range(SPLIT - LAG, SPLIT):
        split_z(i)
    for j in range(CHUNKS):
        finish(0, j)
    for j in range(DIRECT):
        finish(1, j)
    for i in range(SPLIT):
        split_finish(i)

    flat = [copy for group in (*vx, *vz, *vxr, *vzr, *cx, *zf) for copy in group]
    for copy in (*flat, *ay, *ayr, vs, as_, *xf, *zc[:DIRECT]):
        copy.wait_send()

    @pl.when(core == 0)
    def _():
        for copy in zc[DIRECT:]:
            copy.wait_send()

    @pl.when(core == 1)
    def _():
        for copy in zf2:
            copy.wait_send()

    @pl.when(leaves)
    def _():
        for copy in crossf:
            copy.wait_send()

    @pl.when(stays & (core == 0))
    def _():
        for copy in keepf:
            copy.wait_send()

    for t in range(2):
        @pl.when(leaves)
        def _():
            for copy in cross[t]:
                copy.wait_send()

        @pl.when(stays & (core != t))
        def _():
            for copy in keep[t]:
                copy.wait_send()


def fast_body(moments, eigen_basis, slot_order):
    rows, cols = moments.shape
    f32 = jnp.float32
    chunk = rows // CHUNKS
    wide_half = cols // 2
    return pl.pallas_call(
        kernel,
        out_shape=jax.ShapeDtypeStruct((rows, wide_half), f32),
        in_specs=[
            pl.BlockSpec(memory_space=pltpu.SMEM),
            pl.BlockSpec(memory_space=pl.ANY),
            pl.BlockSpec(memory_space=pl.ANY),
        ],
        out_specs=pl.BlockSpec(memory_space=pltpu.VMEM),
        scratch_shapes=[
            pltpu.VMEM((4, rows, cols), f32),
            pltpu.VMEM((4, 2, rows, cols), jnp.bfloat16),
            pltpu.VMEM((4, 2, rows, wide_half), f32),
            pltpu.VMEM((2, rows, cols), f32),
            pltpu.VMEM((2, 2, cols, rows), jnp.bfloat16),
            *[pltpu.VMEM((2, CHUNKS, chunk, wide_half), f32)] * 4,
            *[pltpu.VMEM((CHUNKS, chunk, wide_half), f32)] * 4,
            pltpu.VMEM((SPLIT, 2, chunk, wide_half), f32),
            pltpu.VMEM((SPLIT, 2, chunk // 2, wide_half), f32),
            *[pltpu.VMEM((SPLIT, chunk // 2, wide_half), f32)] * 7,
            pltpu.SemaphoreType.DMA((4,)),
            pltpu.SemaphoreType.DMA((COPIES,)),
            pltpu.SemaphoreType.DMA((COPIES,)),
        ],
        compiler_params=pltpu.CompilerParams(
            collective_id=0, has_side_effects=True, vmem_limit_bytes=56 * 1024 * 1024
        ),
        name="rayleigh",
    )(slot_order, moments, eigen_basis)


def partner(value, axis, stride):
    mask = 2**stride
    pairs = [(source, source ^ mask) for source in range(lax.axis_size(axis))]
    return lax.ppermute(value, axis, pairs)


def body(moments, eigen_basis, slot_order):
    wide_pos = lax.axis_index("wide")
    subproblem = wide_pos // GROUP_WIDE
    position = wide_pos % GROUP_WIDE
    swapped = lax.dynamic_index_in_dim(slot_order, subproblem, 0, keepdims=False)
    narrow_pos = lax.axis_index("narrow")
    col_count = eigen_basis.shape[1]
    half_cols = col_count // 2
    full_basis = lax.all_gather(eigen_basis, "narrow", axis=1, tiled=True)
    first_half = lax.dynamic_slice_in_dim(full_basis, narrow_pos * half_cols, half_cols, 1)
    second_half = lax.dynamic_slice_in_dim(full_basis, K + narrow_pos * half_cols, half_cols, 1)
    local_panel = jnp.concatenate([first_half, second_half], axis=1)
    pair_block = partner(local_panel, "wide", 0)
    joined = jnp.where(
        position % 2 == 0,
        jnp.concatenate([local_panel, pair_block], axis=0),
        jnp.concatenate([pair_block, local_panel], axis=0),
    )
    quad_block = partner(joined, "wide", 1)
    col_panel = jnp.where(
        position // 2 % 2 == 0,
        jnp.concatenate([joined, quad_block], axis=0),
        jnp.concatenate([quad_block, joined], axis=0),
    )
    products = jnp.dot(
        lax.all_gather(moments, "narrow", axis=1, tiled=True),
        col_panel,
        precision=lax.Precision.HIGHEST,
        preferred_element_type=jnp.float32,
    )
    partials = []
    for slot_index in range(2):
        half_panel = products[:, slot_index * half_cols : (slot_index + 1) * half_cols]
        vectors_half = full_basis[:, slot_index * K : (slot_index + 1) * K]
        partials.append(
            lax.dot_general(
                vectors_half,
                half_panel,
                (((0,), (0,)), ((), ())),
                precision=lax.Precision.HIGHEST,
                preferred_element_type=jnp.float32,
            )
        )
    stacked = jnp.stack(partials)
    slot_pick = (position // 2 + swapped) % 2
    row_part = position % 2
    summed = stacked + partner(stacked, "wide", 0)
    summed = summed + partner(summed, "wide", 1)
    chosen = lax.dynamic_index_in_dim(summed, slot_pick, 0, keepdims=False)
    return lax.dynamic_slice_in_dim(chosen, row_part * (K // 2), K // 2, 0)


def solution(mesh):
    placed = (P("wide", "narrow"), P("wide", "narrow"), P())
    cube = mesh.shape["narrow"] == 4
    return jax.shard_map(
        fast_body if cube else body, mesh=mesh, in_specs=placed, out_specs=P("wide", "narrow"), check_vma=False
    )
```
